256 devices in a mesh: grp: 4 (over x), dev: 64 (over z, y, core).
Axes of the slice: x: 4, y: 4, z: 8, core: 2. Of those that a mesh axis runs over, the one named last changes fastest.
Arguments:
- node_feat: bfloat16 [524288, 256], P(('grp', 'dev')), may hold values from -6 to 6
- send_node: int32 [256, 256, 16], P(('grp', 'dev')), may hold values from 0 to 2047, as said below
- pin_net: int32 [256, 256, 16], P(('grp', 'dev')), may hold values from 0 to 1023, as said below
- pin_count: int32 [256, 256], P(('grp', 'dev')), may hold values from 4 to 16, as said below
- pin_w1: bfloat16 [256, 512], replicated, may hold values from -0.375 to 0.375
- pin_b1: float32 [512], replicated, may hold values from -4 to 4
- pin_w2: bfloat16 [512, 256], replicated, may hold values from -0.25 to 0.25
- net_w1: bfloat16 [256, 512], replicated, may hold values from -0.375 to 0.375
- net_b1: float32 [512], replicated, may hold values from -4 to 4
- net_w2: bfloat16 [512, 256], replicated, may hold values from -0.25 to 0.25
- self_w: bfloat16 [256, 512], replicated, may hold values from -0.375 to 0.375
- msg_w: bfloat16 [256, 512], replicated, may hold values from -0.375 to 0.375
- node_b: float32 [512], replicated, may hold values from -4 to 4
- out_w: bfloat16 [512, 256], replicated, may hold values from -0.25 to 0.25
Outputs:
- updated: bfloat16 [524288, 256], P(('grp', 'dev'))
The draws below stay inside these ranges and needn't reach their ends.
Inputs may be any that keep to these rules, and one draw needn't show every extreme that they name: `send_node`: slots at or past the count hold arbitrary local nodes. `pin_net`: every net of every owner has at least one live pin; slots at or past the count hold arbitrary local nets. `pin_count`: in every draw each net owner receives 16 live slots from some device, and some net owner receives 16 live slots from every device.
All inputs are finite; a program needn't handle non-finite values.
Results may differ from the reference program's by a relative error of at most 0.0055.
Values may be sent and summed in bfloat16 or wider, within the bound.
A program may use at most 64 MiB of HBM per device.

```python
import jax
import jax.numpy as jnp
from jax import lax

H = 256
FF = 512
NODE_DEV = 2048
NET_DEV = 1024
OWNERS = 256
PAIR_SLOTS = 16
NODES = 524288


def pin_tables(key):
    base = jax.random.fold_in(key, 7)
    key_count, key_full, key_row, key_thin, key_perm, key_extra, key_node = jax.random.split(base, 7)
    lowest = NET_DEV // OWNERS
    counts = jax.random.randint(key_count, (OWNERS, OWNERS), lowest, PAIR_SLOTS + 1, dtype=jnp.int32)
    columns = jnp.arange(OWNERS, dtype=jnp.int32)[None, :]
    row_index = jnp.arange(OWNERS, dtype=jnp.int32)[:, None]
    full_src = jax.random.randint(key_full, (OWNERS,), 0, OWNERS, dtype=jnp.int32)
    counts = jnp.where(columns == full_src[:, None], PAIR_SLOTS, counts)
    full_dst = jax.random.randint(key_row, (), 0, OWNERS, dtype=jnp.int32)
    counts = jnp.where(row_index == full_dst, PAIR_SLOTS, counts)
    thin_src = jax.random.randint(key_thin, (), 0, OWNERS, dtype=jnp.int32)
    thin_dst = (full_dst + 1) % OWNERS
    counts = jnp.where((row_index == thin_dst) & (columns == thin_src) & (columns != full_src[:, None]), lowest, counts)
    offsets = jnp.cumsum(counts, axis=1) - counts
    ranks = offsets[:, :, None] + jnp.arange(PAIR_SLOTS, dtype=jnp.int32)[None, None, :]
    orders = jax.vmap(lambda subkey: jax.random.permutation(subkey, NET_DEV))(jax.random.split(key_perm, OWNERS)).astype(jnp.int32)
    clipped = jnp.minimum(ranks, NET_DEV - 1).reshape(OWNERS, -1)
    first_nets = jnp.take_along_axis(orders, clipped, axis=1).reshape(ranks.shape)
    extra_nets = jax.random.randint(key_extra, (OWNERS, OWNERS, PAIR_SLOTS), 0, NET_DEV, dtype=jnp.int32)
    net_table = jnp.where(ranks < NET_DEV, first_nets, extra_nets).astype(jnp.int32)
    node_table = jax.random.randint(key_node, (OWNERS, OWNERS, PAIR_SLOTS), 0, NODE_DEV, dtype=jnp.int32)
    return (counts.astype(jnp.int32), net_table, node_table)


def draw_send_node(key, part):
    counts, net_table, node_table = pin_tables(key)
    return jnp.transpose(node_table, (1, 0, 2))


def draw_pin_net(key, part):
    counts, net_table, node_table = pin_tables(key)
    return net_table


def draw_pin_count(key, part):
    counts, net_table, node_table = pin_tables(key)
    return counts


def level_of(key, extent, cuts, smallest, top_value):
    def one(position, parts):
        draws = jax.random.uniform(jax.random.fold_in(jax.random.fold_in(key, 6), position), (parts,), jnp.float32, smallest / len(cuts), top_value / len(cuts))
        return jnp.repeat(jnp.exp(draws), extent[position] // parts).reshape((-1,) + (1,) * (len(extent) - position - 1))

    factor_of = one(*cuts[0])
    for cut in cuts[1:]:
        factor_of = factor_of * one(*cut)
    return factor_of


def gaussian(stream_key, dims, deviation, bound, shards=(), kind=jnp.bfloat16):
    loudness = level_of(stream_key, dims, shards, -0.22, 0.18) if shards else 1.0
    drawn = jax.random.normal(stream_key, dims, jnp.float32) * deviation * loudness
    return jnp.minimum(jnp.maximum(drawn, -bound), bound).astype(kind)


def setup_inputs(seed: int = 0) -> dict:
    streams_of = jax.random.split(jax.random.key(seed), 15)
    node_feat = gaussian(streams_of[0], (NODES, H), 1.0, 6.0, ((0, 256),))
    send_node = draw_send_node(jax.random.fold_in(streams_of[14], 71), 0)
    pin_net = draw_pin_net(jax.random.fold_in(streams_of[14], 71), 0)
    pin_count = draw_pin_count(jax.random.fold_in(streams_of[14], 71), 0)
    pin_w1 = gaussian(streams_of[4], (H, FF), H ** -0.5, 0.375)
    pin_b1 = gaussian(streams_of[5], (FF,), 1.0, 4.0, (), jnp.float32)
    pin_w2 = gaussian(streams_of[6], (FF, H), FF ** -0.5, 0.25)
    net_w1 = gaussian(streams_of[7], (H, FF), H ** -0.5, 0.375)
    net_b1 = gaussian(streams_of[8], (FF,), 1.0, 4.0, (), jnp.float32)
    net_w2 = gaussian(streams_of[9], (FF, H), FF ** -0.5, 0.25)
    self_w = gaussian(streams_of[10], (H, FF), H ** -0.5, 0.375)
    msg_w = gaussian(streams_of[11], (H, FF), H ** -0.5, 0.375)
    node_b = gaussian(streams_of[12], (FF,), 1.0, 4.0, (), jnp.float32)
    out_w = gaussian(streams_of[13], (FF, H), FF ** -0.5, 0.25)
    return dict(node_feat=node_feat, send_node=send_node, pin_net=pin_net, pin_count=pin_count, pin_w1=pin_w1, pin_b1=pin_b1, pin_w2=pin_w2, net_w1=net_w1, net_b1=net_b1, net_w2=net_w2, self_w=self_w, msg_w=msg_w, node_b=node_b, out_w=out_w)


def pin_transform(node_rows, pin_w1, pin_b1, pin_w2):
    hidden_act = jax.nn.gelu(jnp.dot(node_rows, pin_w1, preferred_element_type=jnp.float32) + pin_b1.astype(jnp.float32))
    return jnp.dot(hidden_act.astype(jnp.bfloat16), pin_w2, preferred_element_type=jnp.float32).astype(jnp.bfloat16)


def reference(node_feat, send_node, pin_net, pin_count, pin_w1, pin_b1, pin_w2, net_w1, net_b1, net_w2, self_w, msg_w, node_b, out_w):
    blocks = node_feat.reshape(OWNERS, NODE_DEV, H)
    pin_feat = lax.map(lambda node_rows: pin_transform(node_rows, pin_w1, pin_b1, pin_w2), blocks).reshape(NODES, H)
    owners = (jnp.arange(OWNERS, dtype=jnp.int32) * NODE_DEV).astype(jnp.int32)
    node_ids = (jnp.transpose(send_node, (1, 0, 2)) + owners[None, :, None]).astype(jnp.int32)
    slot_iota = jnp.arange(PAIR_SLOTS, dtype=jnp.int32)

    def accumulate(node_total, inputs):
        pin_nodes, pin_nets, counts = inputs
        live_mask = (slot_iota[None, :] < counts[:, None]).reshape(-1)
        pin_nodes = pin_nodes.reshape(-1)
        pin_nets = pin_nets.reshape(-1)
        pin_rows = jnp.take(pin_feat, pin_nodes, axis=0).astype(jnp.float32)
        pin_rows = jnp.where(live_mask[:, None], pin_rows, jnp.zeros((), jnp.float32))
        net_sums = jax.ops.segment_sum(pin_rows, pin_nets, num_segments=NET_DEV)
        net_sizes = jax.ops.segment_sum(live_mask.astype(jnp.float32), pin_nets, num_segments=NET_DEV)
        net_mean = (net_sums / net_sizes[:, None]).astype(jnp.bfloat16)
        net_inner = jax.nn.gelu(jnp.dot(net_mean, net_w1, preferred_element_type=jnp.float32) + net_b1.astype(jnp.float32)).astype(jnp.bfloat16)
        message = jnp.dot(net_inner, net_w2, preferred_element_type=jnp.float32).astype(jnp.bfloat16)
        per_pin = jnp.where(live_mask[:, None], jnp.take(message, pin_nets, axis=0).astype(jnp.float32), jnp.zeros((), jnp.float32))
        return node_total.at[pin_nodes].add(per_pin), None

    node_total, _ = lax.scan(accumulate, jnp.zeros((NODES, H), jnp.float32), (node_ids, pin_net, pin_count))
    node_sum = node_total.astype(jnp.bfloat16).reshape(OWNERS, NODE_DEV, H)

    def update(inputs):
        node_rows, sums_rows = inputs
        pre_act = jnp.dot(node_rows, self_w, preferred_element_type=jnp.float32) + jnp.dot(sums_rows, msg_w, preferred_element_type=jnp.float32) + node_b.astype(jnp.float32)
        node_inner = jax.nn.silu(pre_act).astype(jnp.bfloat16)
        return (node_rows.astype(jnp.float32) + jnp.dot(node_inner, out_w, preferred_element_type=jnp.float32)).astype(jnp.bfloat16)

    return lax.map(update, (blocks, node_sum)).reshape(NODES, H)
```

```python
import functools

import jax
import jax.numpy as jnp
from jax import lax
from jax.experimental import pallas as pl
from jax.experimental.pallas import tpu as pltpu
from jax.sharding import PartitionSpec as P

MESH = pl.DeviceIdType.MESH
BF16 = jnp.bfloat16
F32 = jnp.float32

XS = 4
ZS = 8
QS = 8
SLOTS = 16
PEERS = XS * QS
CHUNK = PEERS * SLOTS
NODES = 2048
NETS = 1024
H = 256
FF = 512


def dot(a, b):
    return jnp.dot(a, b, preferred_element_type=F32)


def chunk_offset(step):
    return 4 + (1 - 2 * lax.rem(step, 2)) * lax.div(step + 1, 2)


def select_rows(table, ids_ref, plane, count):
    picked = []
    for part in range(XS):
        ids = ids_ref[plane, pl.ds(part, 1), :]
        columns = jnp.transpose(jnp.broadcast_to(ids, (128, 128)))
        columns = jnp.concatenate([columns] * (count // 128), axis=1)
        places = lax.broadcasted_iota(jnp.int32, (128, count), 1)
        picked.append(jnp.where(columns == places, 1.0, 0.0).astype(BF16))
    return dot(jnp.concatenate(picked, axis=0), table)


def onehot_t(ids_ref, plane, base, count):
    ids = jnp.concatenate([ids_ref[plane, pl.ds(part, 1), :] for part in range(XS)], axis=1)
    places = lax.broadcasted_iota(jnp.int32, (count, CHUNK), 0) + base
    return jnp.where(ids == places, 1.0, 0.0).astype(BF16)


def layer_kernel(
    x_ref, node_ids, net_ids,
    pin_w1, pin_b1, pin_w2, net_w1, net_b1, net_w2, self_w, msg_w, node_b, out_w,
    o_ref,
    table, out1, in1, out2, in2, net_acc, net_inv, node_acc, self_part,
    send1, recv1, send2, recv2,
):
    x = lax.axis_index("grp")
    dev = lax.axis_index("dev")
    z = lax.div(dev, QS)
    q = lax.rem(dev, QS)

    barrier = pltpu.get_barrier_semaphore()
    for dx in range(XS):
        tx = lax.rem(x + dx, XS)

        @pl.loop(0, ZS)
        def _(dz, tx=tx, dx=dx):
            tz = lax.rem(z + dz, ZS)
            for dq in range(QS):
                target = (tx, tz * QS + lax.rem(q + dq, QS))
                if dx or dq:
                    pl.semaphore_signal(barrier, inc=1, device_id=target, device_id_type=MESH)
                else:
                    @pl.when(dz > 0)
                    def _(target=target):
                        pl.semaphore_signal(barrier, inc=1, device_id=target, device_id_type=MESH)

    @pl.loop(0, NODES // 256)
    def _(tile):
        rows = pl.ds(pl.multiple_of(tile * 256, 256), 256)
        inner = jax.nn.gelu(dot(x_ref[rows, :], pin_w1[...]) + pin_b1[...])
        table[rows, :] = dot(inner.astype(BF16), pin_w2[...]).astype(BF16)

    def send_plane(src, dst, send_sem, recv_sem, tz, first):
        @pl.loop(0, XS)
        def _(dx):
            tx = lax.rem(x + dx, XS)
            for dq in range(QS):
                tq = lax.rem(q + dq, QS)

                def start(tx=tx, tq=tq):
                    pltpu.make_async_remote_copy(
                        src_ref=src.at[tz, tx * QS + tq],
                        dst_ref=dst.at[z, x * QS + q],
                        send_sem=send_sem.at[tz],
                        recv_sem=recv_sem.at[z],
                        device_id=(tx, tz * QS + tq),
                        device_id_type=MESH,
                    ).start()

                if first and dq == 0:
                    pl.when(dx > 0)(start)
                else:
                    start()

        if first:
            pltpu.make_async_copy(src.at[z, x * QS + q], dst.at[z, x * QS + q], recv_sem.at[z]).start()

    def exchange_out(rows_of, src, dst, send_sem, recv_sem, after_first=None):
        def one(step, first=False):
            tz = lax.rem(z + chunk_offset(step), ZS)
            src[tz] = rows_of(tz).astype(BF16).reshape(PEERS, SLOTS, H)
            send_plane(src, dst, send_sem, recv_sem, tz, first)

        src_z = lax.rem(z + 4, ZS)
        src[src_z] = rows_of(src_z).astype(BF16).reshape(PEERS, SLOTS, H)
        if after_first is not None:
            after_first()
        send_plane(src, dst, send_sem, recv_sem, src_z, False)

        @pl.loop(1, ZS - 1)
        def _(step):
            one(step)

        one(ZS - 1, True)

    def wait_in(dst, recv_sem, plane):
        pltpu.make_async_copy(dst.at[plane], dst.at[plane], recv_sem.at[plane]).wait()

    exchange_out(
        lambda tz: select_rows(table[...], node_ids, tz, NODES), out1, in1, send1, recv1,
        lambda: pl.semaphore_wait(barrier, XS * ZS * QS - 1),
    )

    net_acc[...] = jnp.zeros_like(net_acc)
    net_inv[...] = jnp.zeros_like(net_inv)
    ones = jnp.ones((CHUNK, 128), BF16)

    @pl.loop(0, ZS)
    def _(plane):
        net_inv[...] += dot(onehot_t(net_ids, plane, 0, NETS), ones)

    net_inv[...] = 1.0 / net_inv[...]

    @pl.loop(0, NODES // 256)
    def _(tile):
        rows = pl.ds(pl.multiple_of(tile * 256, 256), 256)
        self_part[rows, :] = dot(x_ref[rows, :], self_w[...]) + node_b[...]

    node_acc[...] = jnp.zeros_like(node_acc)

    @pl.loop(0, ZS)
    def _(step):
        sz = lax.rem(z + ZS - chunk_offset(step), ZS)
        wait_in(in1, recv1, sz)
        net_acc[...] += dot(onehot_t(net_ids, sz, 0, NETS), in1[sz].reshape(CHUNK, H))

    @pl.loop(0, NETS // 256)
    def _(tile):
        rows = pl.ds(pl.multiple_of(tile * 256, 256), 256)
        inv = net_inv[rows, :]
        mean = (net_acc[rows, :] * jnp.concatenate([inv, inv], axis=1)).astype(BF16)
        inner = jax.nn.gelu(dot(mean, net_w1[...]) + net_b1[...])
        table[rows, :] = dot(inner.astype(BF16), net_w2[...]).astype(BF16)

    exchange_out(
        lambda tz: select_rows(table[pl.ds(0, NETS), :], net_ids, tz, NETS), out2, in2, send2, recv2,
    )

    @pl.loop(0, ZS)
    def _(step):
        sz = lax.rem(z + ZS - chunk_offset(step), ZS)
        wait_in(in2, recv2, sz)
        rows = in2[sz].reshape(CHUNK, H)
        for half in range(2):
            part = pl.ds(half * NETS, NETS)
            node_acc[part, :] += dot(onehot_t(node_ids, sz, half * NETS, NETS), rows)

    @pl.loop(0, NODES // 256)
    def _(tile):
        rows = pl.ds(pl.multiple_of(tile * 256, 256), 256)
        pre = self_part[rows, :] + dot(node_acc[rows, :].astype(BF16), msg_w[...])
        inner = jax.nn.silu(pre).astype(BF16)
        o_ref[rows, :] = (x_ref[rows, :].astype(F32) + dot(inner, out_w[...])).astype(BF16)

    for src, send_sem in ((out1, send1), (out2, send2)):
        @pl.loop(1, ZS)
        def _(t, src=src, send_sem=send_sem):
            tz = lax.rem(z + t, ZS)
            pltpu.make_async_copy(src.at[tz], src.at[tz], send_sem.at[tz]).wait()

        part = src.at[z, pl.ds(0, PEERS - 1)]
        pltpu.make_async_copy(part, part, send_sem.at[z]).wait()


def layer(x, node_ids, net_ids, *weights):
    dma8 = pltpu.SemaphoreType.DMA((ZS,))
    rows_buf = pltpu.VMEM((ZS, PEERS, SLOTS, H), BF16)
    return pl.pallas_call(
        layer_kernel,
        out_shape=jax.ShapeDtypeStruct((NODES, H), BF16),
        in_specs=[pl.BlockSpec(memory_space=pltpu.VMEM)] * 13,
        out_specs=pl.BlockSpec(memory_space=pltpu.VMEM),
        scratch_shapes=[
            pltpu.VMEM((NODES, H), BF16),
            rows_buf, rows_buf, rows_buf, rows_buf,
            pltpu.VMEM((NETS, H), F32),
            pltpu.VMEM((NETS, 128), F32),
            pltpu.VMEM((NODES, H), F32),
            pltpu.VMEM((NODES, FF), F32),
            dma8, dma8, dma8, dma8,
        ],
        compiler_params=pltpu.CompilerParams(
            collective_id=0, has_side_effects=True, vmem_limit_bytes=56 * 1024 * 1024
        ),
    )(x, node_ids, net_ids, *weights)


def by_plane(ids):
    return ids.reshape(XS, ZS, QS * SLOTS).transpose(1, 0, 2)


def shards(
    node_feat, send_node, pin_net, pin_count,
    pin_w1, pin_b1, pin_w2, net_w1, net_b1, net_w2, self_w, msg_w, node_b, out_w,
):
    slots = lax.broadcasted_iota(jnp.int32, pin_net.shape, 2)
    live_nets = jnp.where(slots < pin_count[:, :, None], pin_net, -1)
    return layer(
        node_feat, by_plane(send_node), by_plane(live_nets),
        pin_w1, pin_b1[None, :], pin_w2, net_w1, net_b1[None, :], net_w2,
        self_w, msg_w, node_b[None, :], out_w,
    )


def solution(mesh):
    owned = ("grp", "dev")
    in_specs = (P(owned, None), P(owned, None, None), P(owned, None, None), P(owned, None)) + (P(),) * 10
    return jax.shard_map(shards, mesh=mesh, in_specs=in_specs, out_specs=P(owned, None), check_vma=False)
```

```python
import jax
import jax.numpy as jnp
from jax import lax
from jax.experimental import pallas as pl
from jax.experimental.pallas import tpu as pltpu
from jax.sharding import PartitionSpec as P

MESH = pl.DeviceIdType.MESH
BF16 = jnp.bfloat16
F32 = jnp.float32

XS = 4
ZS = 8
QS = 8
SLOTS = 16
PEERS = XS * ZS
CHUNK = PEERS * SLOTS
OWNERS = XS * ZS * QS
NODES = 2048
NETS = 1024
H = 256
FF = 512
TILE = 256
OPERANDS = 14


def dot(a, b):
    return jnp.dot(a, b, preferred_element_type=F32)


def dot_nt(a, b):
    return lax.dot_general(a, b, (((1,), (1,)), ((), ())), preferred_element_type=F32)


def offset(step):
    return 4 + (1 - 2 * lax.rem(step, 2)) * lax.div(step + 1, 2)


def iota(shape, axis):
    return lax.broadcasted_iota(jnp.int32, shape, axis)


def split_ids(ids):
    high = lax.shift_right_logical(ids, 8)
    low = lax.bitwise_and(ids, 255)
    return jnp.concatenate([high, low], axis=0).astype(F32).astype(BF16)


def chunk_digits(digits, q):
    pin = iota((CHUNK, OWNERS), 0)
    owner = lax.div(pin, ZS * SLOTS) * (ZS * QS) + lax.rem(lax.div(pin, SLOTS), ZS) * QS
    take = jnp.where(iota((CHUNK, OWNERS), 1) - q == owner, 1.0, 0.0).astype(BF16)
    spread = dot_nt(take, digits)
    own_slot = lax.rem(iota((CHUNK, 2 * SLOTS), 1), SLOTS) == lax.rem(iota((CHUNK, 2 * SLOTS), 0), SLOTS)
    return jnp.where(own_slot, spread, 0.0).astype(BF16)


def ids_down(digits, q):
    weights = jnp.where(iota((2 * SLOTS, 128), 0) < SLOTS, 256.0, 1.0).astype(BF16)
    return dot(chunk_digits(digits, q), weights).astype(jnp.int32)


def ids_across(digits, q):
    weights = jnp.where(iota((8, 2 * SLOTS), 1) < SLOTS, 256.0, 1.0).astype(BF16)
    return dot_nt(weights, chunk_digits(digits, q))[0:1, :].astype(jnp.int32)


def select_rows(table, digits, q, count):
    ids = jnp.concatenate([ids_down(digits, q)] * (count // 128), axis=1)
    picked = jnp.where(ids == iota((CHUNK, count), 1), 1.0, 0.0).astype(BF16)
    return dot(picked, table).astype(BF16).reshape(PEERS, SLOTS, H)


def members(ids, base, count):
    return jnp.where(ids == iota((count, CHUNK), 0) + base, 1.0, 0.0).astype(BF16)


def layer_kernel(*refs):
    hbm, o_ref, vmem = refs[:OPERANDS], refs[OPERANDS], refs[OPERANDS + 1 : 2 * OPERANDS + 1]
    (
        table, out1, in1, out2, in2, net_acc, net_inv, node_acc, self_part, node_digits, net_digits,
        load, send1, recv1, send2, recv2, column_sem,
    ) = refs[2 * OPERANDS + 1 :]
    (
        node_ids, x_ref, pin_w1, pin_b1, pin_w2, net_ids, counts,
        net_w1, net_b1, net_w2, self_w, msg_w, node_b, out_w,
    ) = vmem
    x = lax.axis_index("grp")
    dev = lax.axis_index("dev")
    z = lax.div(dev, QS)
    q = lax.rem(dev, QS)
    place = x * ZS + z

    loads = [pltpu.make_async_copy(a, b, load.at[i]) for i, (a, b) in enumerate(zip(hbm, vmem))]
    for copy in loads:
        copy.start()

    def signal(sem, dx, dz, dq):
        target = (lax.rem(x + dx, XS), lax.rem(z + dz, ZS) * QS + lax.rem(q + dq, QS))
        pl.semaphore_signal(sem, inc=1, device_id=target, device_id_type=MESH)

    barrier = pltpu.get_barrier_semaphore()
    for dz in (4, 3, 5, 2, 6, 1, 7):
        signal(barrier, 0, dz, 0)
    for dx in range(XS):
        for dq in range(QS):
            if dx or dq:
                signal(barrier, dx, 0, dq)

    def rows_of(tile):
        return pl.ds(pl.multiple_of(tile * TILE, TILE), TILE)

    def transform(tile):
        rows = rows_of(tile)
        inner = jax.nn.gelu(dot(x_ref[rows, :], pin_w1[...]) + pin_b1[...])
        table[rows, :] = dot(inner.astype(BF16), pin_w2[...]).astype(BF16)

    for copy in loads[:5]:
        copy.wait()
    node_digits[...] = split_ids(node_ids[...])
    pl.loop(0, 6)(transform)
    pl.semaphore_wait(barrier, XS * QS - 1 + ZS - 1)
    for dz in (4, 3, 5, 2, 6, 1, 7):
        signal(column_sem, 0, dz, 0)
    pl.loop(6, NODES // TILE)(transform)

    def send_chunk(src, dst, send_sem, recv_sem, tq, own):
        for dz in (4, 3, 5, 2, 6, 1, 7, 0):
            tz = lax.rem(z + dz, ZS)
            for dx in range(XS):
                tx = lax.rem(x + dx, XS)
                if own and dz == 0 and dx == 0:
                    pltpu.make_async_copy(src.at[q, place], dst.at[q, place], recv_sem.at[q]).start()
                else:
                    pltpu.make_async_remote_copy(
                        src_ref=src.at[tq, tx * ZS + tz],
                        dst_ref=dst.at[q, place],
                        send_sem=send_sem.at[tq],
                        recv_sem=recv_sem.at[q],
                        device_id=(tx, tz * QS + tq),
                        device_id_type=MESH,
                    ).start()

    def exchange_out(rows_for, src, dst, send_sem, recv_sem, before_send=None):
        first_q = lax.rem(q + 4, QS)
        src[first_q] = rows_for(first_q)
        if before_send is not None:
            before_send()
        send_chunk(src, dst, send_sem, recv_sem, first_q, False)

        @pl.loop(1, QS - 1)
        def _(step):
            tq = lax.rem(q + offset(step), QS)
            src[tq] = rows_for(tq)
            send_chunk(src, dst, send_sem, recv_sem, tq, False)

        src[q] = rows_for(q)
        send_chunk(src, dst, send_sem, recv_sem, q, True)

    exchange_out(
        lambda tq: select_rows(table[...], node_digits[...], tq, NODES), out1, in1, send1, recv1,
        lambda: pl.semaphore_wait(column_sem, ZS - 1),
    )

    for copy in loads[5:]:
        copy.wait()
    live = iota((SLOTS, OWNERS), 0) < counts[...]
    net_digits[...] = split_ids(jnp.where(live, net_ids[...], 4095))
    net_acc[...] = jnp.zeros_like(net_acc)
    net_inv[...] = jnp.zeros_like(net_inv)
    node_acc[...] = jnp.zeros_like(node_acc)
    ones = jnp.ones((CHUNK, 128), BF16)

    @pl.loop(0, QS)
    def _(part):
        net_inv[...] += dot(members(ids_across(net_digits[...], part), 0, NETS), ones)

    net_inv[...] = 1.0 / net_inv[...]

    @pl.loop(0, NODES // TILE)
    def _(tile):
        rows = rows_of(tile)
        self_part[rows, :] = dot(x_ref[rows, :], self_w[...]) + node_b[...]

    def wait_in(dst, recv_sem, part):
        pltpu.make_async_copy(dst.at[part], dst.at[part], recv_sem.at[part]).wait()

    @pl.loop(0, QS)
    def _(step):
        sq = lax.rem(q + QS - offset(step), QS)
        picked = members(ids_across(net_digits[...], sq), 0, NETS)
        wait_in(in1, recv1, sq)
        net_acc[...] += dot(picked, in1[sq].reshape(CHUNK, H))

    @pl.loop(0, NETS // TILE)
    def _(tile):
        rows = rows_of(tile)
        inv = net_inv[rows, :]
        mean = (net_acc[rows, :] * jnp.concatenate([inv, inv], axis=1)).astype(BF16)
        inner = jax.nn.gelu(dot(mean, net_w1[...]) + net_b1[...])
        table[rows, :] = dot(inner.astype(BF16), net_w2[...]).astype(BF16)

    exchange_out(
        lambda tq: select_rows(table[pl.ds(0, NETS), :], net_digits[...], tq, NETS), out2, in2, send2, recv2,
    )

    @pl.loop(0, QS)
    def _(step):
        sq = lax.rem(q + QS - offset(step), QS)
        ids = ids_across(node_digits[...], sq)
        wait_in(in2, recv2, sq)
        rows = in2[sq].reshape(CHUNK, H)
        for half in range(2):
            part = pl.ds(half * NETS, NETS)
            node_acc[part, :] += dot(members(ids, half * NETS, NETS), rows)

    @pl.loop(0, NODES // TILE)
    def _(tile):
        rows = rows_of(tile)
        pre = self_part[rows, :] + dot(node_acc[rows, :].astype(BF16), msg_w[...])
        inner = jax.nn.silu(pre).astype(BF16)
        o_ref[rows, :] = (x_ref[rows, :].astype(F32) + dot(inner, out_w[...])).astype(BF16)

    for src, send_sem in ((out1, send1), (out2, send2)):
        @pl.loop(1, QS)
        def _(t, src=src, send_sem=send_sem):
            tq = lax.rem(q + t, QS)
            pltpu.make_async_copy(src.at[tq], src.at[tq], send_sem.at[tq]).wait()

        sent = src.at[q, pl.ds(0, PEERS - 1)]
        pltpu.make_async_copy(sent, sent, send_sem.at[q]).wait()


def layer(*operands):
    loads = pltpu.SemaphoreType.DMA((OPERANDS,))
    eight = pltpu.SemaphoreType.DMA((QS,))
    rows_buf = pltpu.VMEM((QS, PEERS, SLOTS, H), BF16)
    digits = pltpu.VMEM((2 * SLOTS, OWNERS), BF16)
    return pl.pallas_call(
        layer_kernel,
        out_shape=jax.ShapeDtypeStruct((NODES, H), BF16),
        in_specs=[pl.BlockSpec(memory_space=pltpu.HBM)] * OPERANDS,
        out_specs=pl.BlockSpec(memory_space=pltpu.VMEM),
        scratch_shapes=[pltpu.VMEM(a.shape, a.dtype) for a in operands]
        + [
            pltpu.VMEM((NODES, H), BF16),
            rows_buf, rows_buf, rows_buf, rows_buf,
            pltpu.VMEM((NETS, H), F32),
            pltpu.VMEM((NETS, 128), F32),
            pltpu.VMEM((NODES, H), F32),
            pltpu.VMEM((NODES, FF), F32),
            digits, digits,
            loads, eight, eight, eight, eight,
            pltpu.SemaphoreType.REGULAR,
        ],
        compiler_params=pltpu.CompilerParams(
            collective_id=0, has_side_effects=True, vmem_limit_bytes=56 * 1024 * 1024
        ),
    )(*operands)


def shards(
    node_feat, send_node, pin_net, pin_count,
    pin_w1, pin_b1, pin_w2, net_w1, net_b1, net_w2, self_w, msg_w, node_b, out_w,
):
    return layer(
        send_node[0].T, node_feat, pin_w1, pin_b1[None, :], pin_w2, pin_net[0].T, pin_count,
        net_w1, net_b1[None, :], net_w2, self_w, msg_w, node_b[None, :], out_w,
    )


def solution(mesh):
    owned = ("grp", "dev")
    in_specs = (P(owned, None), P(owned, None, None), P(owned, None, None), P(owned, None)) + (P(),) * 10
    return jax.shard_map(shards, mesh=mesh, in_specs=in_specs, out_specs=P(owned, None), check_vma=False)
```

```python
import jax
import jax.numpy as jnp
from jax import lax
from jax.experimental import pallas as pl
from jax.experimental.pallas import tpu as pltpu
from jax.sharding import PartitionSpec as P

MESH = pl.DeviceIdType.MESH
BF16 = jnp.bfloat16
F32 = jnp.float32

XS = 4
ZS = 8
QS = 8
SLOTS = 16
PEERS = XS * QS
CHUNK = PEERS * SLOTS
OWNERS = XS * ZS * QS
NODES = 2048
NETS = 1024
H = 256
FF = 512
TILE = 256
OPERANDS = 14


def dot(a, b):
    return jnp.dot(a, b, preferred_element_type=F32)


def dot_nt(a, b):
    return lax.dot_general(a, b, (((1,), (1,)), ((), ())), preferred_element_type=F32)


def iota(shape, axis):
    return lax.broadcasted_iota(jnp.int32, shape, axis)


def split_ids(ids):
    high = lax.shift_right_logical(ids, 8)
    low = lax.bitwise_and(ids, 255)
    return jnp.concatenate([high, low], axis=0).astype(F32).astype(BF16)


def chunk_digits(digits, plane):
    pin = iota((CHUNK, OWNERS), 0)
    owner = lax.div(pin, QS * SLOTS) * (ZS * QS) + lax.rem(lax.div(pin, SLOTS), QS)
    take = jnp.where(iota((CHUNK, OWNERS), 1) - plane * QS == owner, 1.0, 0.0).astype(BF16)
    spread = dot_nt(take, digits)
    own_slot = lax.rem(iota((CHUNK, 2 * SLOTS), 1), SLOTS) == lax.rem(iota((CHUNK, 2 * SLOTS), 0), SLOTS)
    return jnp.where(own_slot, spread, 0.0).astype(BF16)


def ids_down(digits, plane):
    weights = jnp.where(iota((2 * SLOTS, 128), 0) < SLOTS, 256.0, 1.0).astype(BF16)
    return dot(chunk_digits(digits, plane), weights).astype(jnp.int32)


def ids_across(digits, plane):
    weights = jnp.where(iota((8, 2 * SLOTS), 1) < SLOTS, 256.0, 1.0).astype(BF16)
    return dot_nt(weights, chunk_digits(digits, plane))[0:1, :].astype(jnp.int32)


def select_rows(table, digits, plane, count):
    ids = jnp.concatenate([ids_down(digits, plane)] * (count // 128), axis=1)
    picked = jnp.where(ids == iota((CHUNK, count), 1), 1.0, 0.0).astype(BF16)
    return dot(picked, table).astype(BF16).reshape(PEERS, SLOTS, H)


def members(ids, base, count):
    return jnp.where(ids == iota((count, CHUNK), 0) + base, 1.0, 0.0).astype(BF16)


def layer_kernel(*refs):
    hbm, o_ref, vmem = refs[:OPERANDS], refs[OPERANDS], refs[OPERANDS + 1 : 2 * OPERANDS + 1]
    (
        table, out1, in1, out2, in2, sums_out, sums_in, messages_in, ids_out, ids_in,
        net_acc, up_acc, down_acc, net_inv, node_acc, self_part, node_digits, net_digits, up_digits, down_digits,
        load, send1, recv1, send2, recv2, send_sums, recv_sums, send_messages, recv_messages, send_ids, recv_ids, column_sem,
    ) = refs[2 * OPERANDS + 1 :]
    (
        node_ids, net_ids, counts, x_ref, pin_w1, pin_b1, pin_w2,
        net_w1, net_b1, net_w2, self_w, msg_w, node_b, out_w,
    ) = vmem
    x = lax.axis_index("grp")
    dev = lax.axis_index("dev")
    z = lax.div(dev, QS)
    q = lax.rem(dev, QS)
    place = x * QS + q

    def plane(dz):
        return lax.rem(z + dz + 2 * ZS, ZS)

    up = (x, plane(1) * QS + q)
    down = (x, plane(-1) * QS + q)

    loads = [pltpu.make_async_copy(a, b, load.at[i]) for i, (a, b) in enumerate(zip(hbm, vmem))]
    for copy in loads:
        copy.start()

    def signal(sem, dx, dz, dq):
        target = (lax.rem(x + dx, XS), plane(dz) * QS + lax.rem(q + dq, QS))
        pl.semaphore_signal(sem, inc=1, device_id=target, device_id_type=MESH)

    barrier = pltpu.get_barrier_semaphore()
    for dz in (4, 3, 5, 2, 6, 1, 7):
        signal(barrier, 0, dz, 0)
    for dx in range(XS):
        for dq in range(QS):
            if dx or dq:
                signal(barrier, dx, 0, dq)

    def rows_of(tile):
        return pl.ds(pl.multiple_of(tile * TILE, TILE), TILE)

    def transform(tile):
        rows = rows_of(tile)
        inner = jax.nn.gelu(dot(x_ref[rows, :], pin_w1[...]) + pin_b1[...])
        table[rows, :] = dot(inner.astype(BF16), pin_w2[...]).astype(BF16)

    for copy in loads[:7]:
        copy.wait()
    node_digits[...] = split_ids(node_ids[...])
    live_ids = jnp.where(iota((SLOTS, OWNERS), 0) < counts[...], net_ids[...], 4095)
    ids_out[...] = live_ids
    net_digits[...] = split_ids(live_ids)
    pl.loop(0, 6)(transform)
    pl.semaphore_wait(barrier, XS * QS - 1 + ZS - 1)
    for dz in (4, 3, 5, 2, 6, 1, 7):
        signal(column_sem, 0, dz, 0)
    pl.loop(6, NODES // TILE)(transform)

    def remote(src, dst, send_sem, recv_sem, device):
        return pltpu.make_async_remote_copy(
            src_ref=src, dst_ref=dst, send_sem=send_sem, recv_sem=recv_sem, device_id=device, device_id_type=MESH
        )

    def send_chunk(src, dst, send_sem, recv_sem, kind, tz, own):
        for dq in range(QS):
            tq = lax.rem(q + dq, QS)
            for dx in range(XS):
                tx = lax.rem(x + dx, XS)
                copy = remote(
                    src.at[kind, tx * QS + tq], dst.at[kind, place], send_sem.at[kind], recv_sem.at[kind], (tx, tz * QS + tq)
                )
                if dx or dq:
                    copy.start()
                else:
                    pl.when(jnp.logical_not(own))(copy.start)
                    pl.when(own)(pltpu.make_async_copy(src.at[kind, place], dst.at[kind, place], recv_sem.at[kind]).start)

    def wait_in(dst, recv_sem, kind):
        pltpu.make_async_copy(dst.at[kind], dst.at[kind], recv_sem.at[kind]).wait()

    def gather_nodes(kind):
        out1[kind] = select_rows(table[...], node_digits[...], plane(kind), NODES)

    @pl.loop(0, 3)
    def _(j):
        far = 3 - j
        gather_nodes(far)

        @pl.when(j == 0)
        def _():
            pl.semaphore_wait(column_sem, ZS - 1)

        send_chunk(out1, in1, send1, recv1, far, plane(far - 1), j == 2)
        gather_nodes(ZS - far)
        send_chunk(out1, in1, send1, recv1, ZS - far, plane(1 - far), j == 2)

    id_copies = (
        remote(ids_out, ids_in.at[0], send_ids.at[0], recv_ids.at[0], up),
        remote(ids_out, ids_in.at[1], send_ids.at[1], recv_ids.at[1], down),
    )
    for copy in id_copies:
        copy.start()

    @pl.loop(0, 2)
    def _(j):
        kind = 4 - 4 * j
        gather_nodes(kind)
        send_chunk(out1, in1, send1, recv1, kind, plane(kind), j == 1)

    up_acc[...] = jnp.zeros_like(up_acc)
    down_acc[...] = jnp.zeros_like(down_acc)
    net_acc[...] = jnp.zeros_like(net_acc)
    net_inv[...] = jnp.zeros_like(net_inv)
    ones = jnp.ones((CHUNK, 128), BF16)

    @pl.loop(0, ZS)
    def _(part):
        net_inv[...] += dot(members(ids_across(net_digits[...], part), 0, NETS), ones)

    net_inv[...] = 1.0 / net_inv[...]
    for copy in id_copies:
        copy.wait_recv()
    down_digits[...] = split_ids(ids_in[0])
    up_digits[...] = split_ids(ids_in[1])

    def add_nets(acc, digits, kind, from_plane):
        picked = members(ids_across(digits[...], from_plane), 0, NETS)
        wait_in(in1, recv1, kind)
        acc[...] += dot(picked, in1[kind].reshape(CHUNK, H))

    @pl.loop(0, 3)
    def _(j):
        far = 3 - j
        add_nets(up_acc, up_digits, far, plane(1 - far))
        add_nets(down_acc, down_digits, ZS - far, plane(far - 1))

    sums_out[0] = up_acc[...].astype(BF16)
    sums_out[1] = down_acc[...].astype(BF16)
    sum_copies = (
        remote(sums_out.at[0], sums_in.at[0], send_sums.at[0], recv_sums.at[0], up),
        remote(sums_out.at[1], sums_in.at[1], send_sums.at[1], recv_sums.at[1], down),
    )
    for copy in sum_copies:
        copy.start()

    for copy in loads[7:]:
        copy.wait()
    node_acc[...] = jnp.zeros_like(node_acc)

    @pl.loop(0, NODES // TILE)
    def _(tile):
        rows = rows_of(tile)
        self_part[rows, :] = dot(x_ref[rows, :], self_w[...]) + node_b[...]

    @pl.loop(0, 2)
    def _(j):
        kind = 4 * j
        add_nets(net_acc, net_digits, kind, plane(-kind))

    for copy in sum_copies:
        copy.wait_recv()

    def message_copies(rows):
        return (
            remote(table.at[rows, :], messages_in.at[0, rows, :], send_messages.at[0], recv_messages.at[0], up),
            remote(table.at[rows, :], messages_in.at[1, rows, :], send_messages.at[1], recv_messages.at[1], down),
        )

    @pl.loop(0, NETS // TILE)
    def _(tile):
        rows = rows_of(tile)
        inv = net_inv[rows, :]
        total = net_acc[rows, :] + sums_in[0, rows, :].astype(F32) + sums_in[1, rows, :].astype(F32)
        mean = (total * jnp.concatenate([inv, inv], axis=1)).astype(BF16)
        inner = jax.nn.gelu(dot(mean, net_w1[...]) + net_b1[...])
        table[rows, :] = dot(inner.astype(BF16), net_w2[...]).astype(BF16)
        for copy in message_copies(rows):
            copy.start()

    @pl.loop(0, 2)
    def _(j):
        kind = 4 - 4 * j
        out2[kind] = select_rows(table[pl.ds(0, NETS), :], net_digits[...], plane(kind), NETS)
        send_chunk(out2, in2, send2, recv2, kind, plane(kind), j == 1)

    for copy in message_copies(pl.ds(0, NETS)):
        copy.wait_recv()

    @pl.loop(0, 3)
    def _(j):
        far = 3 - j
        out2[far] = select_rows(messages_in[1], up_digits[...], plane(1 - far), NETS)
        send_chunk(out2, in2, send2, recv2, far, plane(1 - far), j == 2)
        out2[ZS - far] = select_rows(messages_in[0], down_digits[...], plane(far - 1), NETS)
        send_chunk(out2, in2, send2, recv2, ZS - far, plane(far - 1), j == 2)

    def add_nodes(kind):
        ids = ids_across(node_digits[...], plane(kind))
        wait_in(in2, recv2, kind)
        rows = in2[kind].reshape(CHUNK, H)
        for half in range(2):
            part = pl.ds(half * NETS, NETS)
            node_acc[part, :] += dot(members(ids, half * NETS, NETS), rows)

    @pl.loop(0, 2)
    def _(j):
        add_nodes(4 * j)

    @pl.loop(0, 3)
    def _(j):
        add_nodes(3 - j)
        add_nodes(5 + j)

    @pl.loop(0, NODES // TILE)
    def _(tile):
        rows = rows_of(tile)
        pre = self_part[rows, :] + dot(node_acc[rows, :].astype(BF16), msg_w[...])
        inner = jax.nn.silu(pre).astype(BF16)
        o_ref[rows, :] = (x_ref[rows, :].astype(F32) + dot(inner, out_w[...])).astype(BF16)

    for src, send_sem in ((out1, send1), (out2, send2)):
        for kind in range(ZS):
            sent = src.at[kind, pl.ds(0, PEERS - 1)] if kind in (0, 1, 7) else src.at[kind]
            pltpu.make_async_copy(sent, sent, send_sem.at[kind]).wait()
    for copy in id_copies + sum_copies + message_copies(pl.ds(0, NETS)):
        copy.wait_send()


def layer(*operands):
    loads = pltpu.SemaphoreType.DMA((OPERANDS,))
    eight = pltpu.SemaphoreType.DMA((ZS,))
    pair = pltpu.SemaphoreType.DMA((2,))
    rows_buf = pltpu.VMEM((ZS, PEERS, SLOTS, H), BF16)
    net_rows = pltpu.VMEM((2, NETS, H), BF16)
    net_sums = pltpu.VMEM((NETS, H), F32)
    digits = pltpu.VMEM((2 * SLOTS, OWNERS), BF16)
    return pl.pallas_call(
        layer_kernel,
        out_shape=jax.ShapeDtypeStruct((NODES, H), BF16),
        in_specs=[pl.BlockSpec(memory_space=pltpu.HBM)] * OPERANDS,
        out_specs=pl.BlockSpec(memory_space=pltpu.VMEM),
        scratch_shapes=[pltpu.VMEM(a.shape, a.dtype) for a in operands]
        + [
            pltpu.VMEM((NODES, H), BF16),
            rows_buf, rows_buf, rows_buf, rows_buf,
            net_rows, net_rows, net_rows,
            pltpu.VMEM((SLOTS, OWNERS), jnp.int32),
            pltpu.VMEM((2, SLOTS, OWNERS), jnp.int32),
            net_sums, net_sums, net_sums,
            pltpu.VMEM((NETS, 128), F32),
            pltpu.VMEM((NODES, H), F32),
            pltpu.VMEM((NODES, FF), F32),
            digits, digits, digits, digits,
            loads, eight, eight, eight, eight, pair, pair, pair, pair, pair, pair,
            pltpu.SemaphoreType.REGULAR,
        ],
        compiler_params=pltpu.CompilerParams(
            collective_id=0, has_side_effects=True, vmem_limit_bytes=56 * 1024 * 1024
        ),
    )(*operands)


def shards(
    node_feat, send_node, pin_net, pin_count,
    pin_w1, pin_b1, pin_w2, net_w1, net_b1, net_w2, self_w, msg_w, node_b, out_w,
):
    return layer(
        send_node[0].T, pin_net[0].T, pin_count, node_feat, pin_w1, pin_b1[None, :], pin_w2,
        net_w1, net_b1[None, :], net_w2, self_w, msg_w, node_b[None, :], out_w,
    )


def solution(mesh):
    owned = ("grp", "dev")
    in_specs = (P(owned, None), P(owned, None, None), P(owned, None, None), P(owned, None)) + (P(),) * 10
    return jax.shard_map(shards, mesh=mesh, in_specs=in_specs, out_specs=P(owned, None), check_vma=False)
```

```python
import jax
import jax.numpy as jnp
from jax import lax
from jax.experimental import pallas as pl
from jax.experimental.pallas import tpu as pltpu
from jax.sharding import PartitionSpec as P

MESH = pl.DeviceIdType.MESH
BF16 = jnp.bfloat16
F32 = jnp.float32

XS = 4
ZS = 8
QS = 8
SLOTS = 16
PEERS = XS * QS
CHUNK = PEERS * SLOTS
OWNERS = XS * ZS * QS
NODES = 2048
NETS = 1024
H = 256
FF = 512
TILE = 256
OPERANDS = 14


def dot(a, b):
    return jnp.dot(a, b, preferred_element_type=F32)


def dot_nt(a, b):
    return lax.dot_general(a, b, (((1,), (1,)), ((), ())), preferred_element_type=F32)


def iota(shape, axis):
    return lax.broadcasted_iota(jnp.int32, shape, axis)


def split_ids(ids):
    high = lax.shift_right_logical(ids, 8)
    low = lax.bitwise_and(ids, 255)
    return jnp.concatenate([high, low], axis=0).astype(F32).astype(BF16)


def chunk_digits(digits, plane):
    pin = iota((CHUNK, OWNERS), 0)
    owner = lax.div(pin, QS * SLOTS) * (ZS * QS) + lax.rem(lax.div(pin, SLOTS), QS)
    take = jnp.where(iota((CHUNK, OWNERS), 1) - plane * QS == owner, 1.0, 0.0).astype(BF16)
    spread = dot_nt(take, digits)
    own_slot = lax.rem(iota((CHUNK, 2 * SLOTS), 1), SLOTS) == lax.rem(iota((CHUNK, 2 * SLOTS), 0), SLOTS)
    return jnp.where(own_slot, spread, 0.0).astype(BF16)


def ids_down(digits, plane):
    weights = jnp.where(iota((2 * SLOTS, 128), 0) < SLOTS, 256.0, 1.0).astype(BF16)
    return dot(chunk_digits(digits, plane), weights).astype(jnp.int32)


def ids_across(digits, plane):
    weights = jnp.where(iota((8, 2 * SLOTS), 1) < SLOTS, 256.0, 1.0).astype(BF16)
    return dot_nt(weights, chunk_digits(digits, plane))[0:1, :].astype(jnp.int32)


def select_rows(table, digits, plane, count):
    ids = jnp.concatenate([ids_down(digits, plane)] * (count // 128), axis=1)
    picked = jnp.where(ids == iota((CHUNK, count), 1), 1.0, 0.0).astype(BF16)
    return dot(picked, table).astype(BF16).reshape(PEERS, SLOTS, H)


def members(ids, base, count):
    return jnp.where(ids == iota((count, CHUNK), 0) + base, 1.0, 0.0).astype(BF16)


def layer_kernel(*refs):
    hbm, o_ref, vmem = refs[:OPERANDS], refs[OPERANDS], refs[OPERANDS + 1 : 2 * OPERANDS + 1]
    (
        table, out1, in1, out2, in2, sums_out, sums_in, messages_in, ids_out, ids_in,
        net_acc, up_acc, down_acc, net_inv, node_acc, self_part, node_digits, net_digits, up_digits, down_digits,
        load, send1, recv1, send2, recv2, send_sums, recv_sums, send_messages, recv_messages, send_ids, recv_ids, column_sem,
    ) = refs[2 * OPERANDS + 1 :]
    (
        node_ids, net_ids, counts, x_ref, pin_w1, pin_b1, pin_w2,
        net_w1, net_b1, net_w2, self_w, msg_w, node_b, out_w,
    ) = vmem
    x = lax.axis_index("grp")
    dev = lax.axis_index("dev")
    z = lax.div(dev, QS)
    q = lax.rem(dev, QS)
    place = x * QS + q

    def plane(dz):
        return lax.rem(z + dz + 2 * ZS, ZS)

    up = (x, plane(1) * QS + q)
    down = (x, plane(-1) * QS + q)

    loads = [pltpu.make_async_copy(a, b, load.at[i]) for i, (a, b) in enumerate(zip(hbm, vmem))]
    for copy in loads:
        copy.start()

    def signal(sem, dx, dz, dq):
        target = (lax.rem(x + dx, XS), plane(dz) * QS + lax.rem(q + dq, QS))
        pl.semaphore_signal(sem, inc=1, device_id=target, device_id_type=MESH)

    barrier = pltpu.get_barrier_semaphore()
    for dz in (4, 3, 5, 2, 6, 1, 7):
        signal(barrier, 0, dz, 0)
    for dx in range(XS):
        for dq in range(QS):
            if dx or dq:
                signal(barrier, dx, 0, dq)

    def rows_of(tile):
        return pl.ds(pl.multiple_of(tile * TILE, TILE), TILE)

    def transform(tile):
        rows = rows_of(tile)
        inner = jax.nn.gelu(dot(x_ref[rows, :], pin_w1[...]) + pin_b1[...])
        table[rows, :] = dot(inner.astype(BF16), pin_w2[...]).astype(BF16)

    for copy in loads[:7]:
        copy.wait()
    node_digits[...] = split_ids(node_ids[...])
    live_ids = jnp.where(iota((SLOTS, OWNERS), 0) < counts[...], net_ids[...], 4095)
    ids_out[...] = live_ids
    net_digits[...] = split_ids(live_ids)
    pl.loop(0, 6)(transform)
    pl.semaphore_wait(barrier, XS * QS - 1 + ZS - 1)
    for dz in (4, 3, 5, 2, 6, 1, 7):
        signal(column_sem, 0, dz, 0)
    pl.loop(6, NODES // TILE)(transform)

    def remote(src, dst, send_sem, recv_sem, device):
        return pltpu.make_async_remote_copy(
            src_ref=src, dst_ref=dst, send_sem=send_sem, recv_sem=recv_sem, device_id=device, device_id_type=MESH
        )

    def send_chunk(src, dst, send_sem, recv_sem, kind, tz, own):
        for dx in (2, 1, 3, 0):
            tx = lax.rem(x + dx, XS)
            for dq in (4, 3, 5, 2, 6, 1, 7, 0):
                tq = lax.rem(q + dq, QS)
                copy = remote(
                    src.at[kind, tx * QS + tq], dst.at[kind, place], send_sem.at[kind], recv_sem.at[kind], (tx, tz * QS + tq)
                )
                if dx or dq:
                    copy.start()
                else:
                    pl.when(jnp.logical_not(own))(copy.start)
                    pl.when(own)(pltpu.make_async_copy(src.at[kind, place], dst.at[kind, place], recv_sem.at[kind]).start)

    def wait_in(dst, recv_sem, kind):
        pltpu.make_async_copy(dst.at[kind], dst.at[kind], recv_sem.at[kind]).wait()

    def gather_nodes(kind):
        out1[kind] = select_rows(table[...], node_digits[...], plane(kind), NODES)

    @pl.loop(0, 3)
    def _(j):
        far = 3 - j
        gather_nodes(far)

        @pl.when(j == 0)
        def _():
            pl.semaphore_wait(column_sem, ZS - 1)

        send_chunk(out1, in1, send1, recv1, far, plane(far - 1), j == 2)
        gather_nodes(ZS - far)
        send_chunk(out1, in1, send1, recv1, ZS - far, plane(1 - far), j == 2)

    id_copies = (
        remote(ids_out, ids_in.at[0], send_ids.at[0], recv_ids.at[0], up),
        remote(ids_out, ids_in.at[1], send_ids.at[1], recv_ids.at[1], down),
    )
    for copy in id_copies:
        copy.start()

    @pl.loop(0, 2)
    def _(j):
        kind = 4 - 4 * j
        gather_nodes(kind)
        send_chunk(out1, in1, send1, recv1, kind, plane(kind), j == 1)

    up_acc[...] = jnp.zeros_like(up_acc)
    down_acc[...] = jnp.zeros_like(down_acc)
    net_acc[...] = jnp.zeros_like(net_acc)
    net_inv[...] = jnp.zeros_like(net_inv)
    ones = jnp.ones((CHUNK, 128), BF16)

    @pl.loop(0, ZS)
    def _(part):
        net_inv[...] += dot(members(ids_across(net_digits[...], part), 0, NETS), ones)

    net_inv[...] = 1.0 / net_inv[...]
    for copy in id_copies:
        copy.wait_recv()
    down_digits[...] = split_ids(ids_in[0])
    up_digits[...] = split_ids(ids_in[1])

    def add_nets(acc, digits, kind, from_plane):
        picked = members(ids_across(digits[...], from_plane), 0, NETS)
        wait_in(in1, recv1, kind)
        acc[...] += dot(picked, in1[kind].reshape(CHUNK, H))

    @pl.loop(0, 3)
    def _(j):
        far = 3 - j
        add_nets(up_acc, up_digits, far, plane(1 - far))
        add_nets(down_acc, down_digits, ZS - far, plane(far - 1))

    sums_out[0] = up_acc[...].astype(BF16)
    sums_out[1] = down_acc[...].astype(BF16)
    sum_copies = (
        remote(sums_out.at[0], sums_in.at[0], send_sums.at[0], recv_sums.at[0], up),
        remote(sums_out.at[1], sums_in.at[1], send_sums.at[1], recv_sums.at[1], down),
    )
    for copy in sum_copies:
        copy.start()

    for copy in loads[7:]:
        copy.wait()
    node_acc[...] = jnp.zeros_like(node_acc)

    @pl.loop(0, NODES // TILE)
    def _(tile):
        rows = rows_of(tile)
        self_part[rows, :] = dot(x_ref[rows, :], self_w[...]) + node_b[...]

    @pl.loop(0, 2)
    def _(j):
        kind = 4 * j
        add_nets(net_acc, net_digits, kind, plane(-kind))

    for copy in sum_copies:
        copy.wait_recv()

    def message_copies(rows):
        return (
            remote(table.at[rows, :], messages_in.at[0, rows, :], send_messages.at[0], recv_messages.at[0], up),
            remote(table.at[rows, :], messages_in.at[1, rows, :], send_messages.at[1], recv_messages.at[1], down),
        )

    @pl.loop(0, NETS // TILE)
    def _(tile):
        rows = rows_of(tile)
        inv = net_inv[rows, :]
        total = net_acc[rows, :] + sums_in[0, rows, :].astype(F32) + sums_in[1, rows, :].astype(F32)
        mean = (total * jnp.concatenate([inv, inv], axis=1)).astype(BF16)
        inner = jax.nn.gelu(dot(mean, net_w1[...]) + net_b1[...])
        table[rows, :] = dot(inner.astype(BF16), net_w2[...]).astype(BF16)
        for copy in message_copies(rows):
            copy.start()

    @pl.loop(0, 2)
    def _(j):
        kind = 4 - 4 * j
        out2[kind] = select_rows(table[pl.ds(0, NETS), :], net_digits[...], plane(kind), NETS)
        send_chunk(out2, in2, send2, recv2, kind, plane(kind), j == 1)

    for copy in message_copies(pl.ds(0, NETS)):
        copy.wait_recv()

    @pl.loop(0, 3)
    def _(j):
        far = 3 - j
        out2[far] = select_rows(messages_in[1], up_digits[...], plane(1 - far), NETS)
        send_chunk(out2, in2, send2, recv2, far, plane(1 - far), j == 2)
        out2[ZS - far] = select_rows(messages_in[0], down_digits[...], plane(far - 1), NETS)
        send_chunk(out2, in2, send2, recv2, ZS - far, plane(far - 1), j == 2)

    def add_nodes(kind):
        ids = ids_across(node_digits[...], plane(kind))
        wait_in(in2, recv2, kind)
        rows = in2[kind].reshape(CHUNK, H)
        for half in range(2):
            part = pl.ds(half * NETS, NETS)
            node_acc[part, :] += dot(members(ids, half * NETS, NETS), rows)

    @pl.loop(0, 2)
    def _(j):
        add_nodes(4 * j)

    @pl.loop(0, 3)
    def _(j):
        add_nodes(3 - j)
        add_nodes(5 + j)

    @pl.loop(0, NODES // TILE)
    def _(tile):
        rows = rows_of(tile)
        pre = self_part[rows, :] + dot(node_acc[rows, :].astype(BF16), msg_w[...])
        inner = (0.5 * pre * (1.0 + jnp.tanh(0.5 * pre))).astype(BF16)
        o_ref[rows, :] = (x_ref[rows, :].astype(F32) + dot(inner, out_w[...])).astype(BF16)

    for src, send_sem in ((out1, send1), (out2, send2)):
        for kind in range(ZS):
            sent = src.at[kind, pl.ds(0, PEERS - 1)] if kind in (0, 1, 7) else src.at[kind]
            pltpu.make_async_copy(sent, sent, send_sem.at[kind]).wait()
    for copy in id_copies + sum_copies + message_copies(pl.ds(0, NETS)):
        copy.wait_send()


def layer(*operands):
    loads = pltpu.SemaphoreType.DMA((OPERANDS,))
    eight = pltpu.SemaphoreType.DMA((ZS,))
    pair = pltpu.SemaphoreType.DMA((2,))
    rows_buf = pltpu.VMEM((ZS, PEERS, SLOTS, H), BF16)
    net_rows = pltpu.VMEM((2, NETS, H), BF16)
    net_sums = pltpu.VMEM((NETS, H), F32)
    digits = pltpu.VMEM((2 * SLOTS, OWNERS), BF16)
    return pl.pallas_call(
        layer_kernel,
        out_shape=jax.ShapeDtypeStruct((NODES, H), BF16),
        in_specs=[pl.BlockSpec(memory_space=pltpu.HBM)] * OPERANDS,
        out_specs=pl.BlockSpec(memory_space=pltpu.VMEM),
        scratch_shapes=[pltpu.VMEM(a.shape, a.dtype) for a in operands]
        + [
            pltpu.VMEM((NODES, H), BF16),
            rows_buf, rows_buf, rows_buf, rows_buf,
            net_rows, net_rows, net_rows,
            pltpu.VMEM((SLOTS, OWNERS), jnp.int32),
            pltpu.VMEM((2, SLOTS, OWNERS), jnp.int32),
            net_sums, net_sums, net_sums,
            pltpu.VMEM((NETS, 128), F32),
            pltpu.VMEM((NODES, H), F32),
            pltpu.VMEM((NODES, FF), F32),
            digits, digits, digits, digits,
            loads, eight, eight, eight, eight, pair, pair, pair, pair, pair, pair,
            pltpu.SemaphoreType.REGULAR,
        ],
        compiler_params=pltpu.CompilerParams(
            collective_id=0, has_side_effects=True, vmem_limit_bytes=56 * 1024 * 1024
        ),
    )(*operands)


def shards(
    node_feat, send_node, pin_net, pin_count,
    pin_w1, pin_b1, pin_w2, net_w1, net_b1, net_w2, self_w, msg_w, node_b, out_w,
):
    return layer(
        send_node[0].T, pin_net[0].T, pin_count, node_feat, pin_w1, pin_b1[None, :], pin_w2,
        net_w1, net_b1[None, :], net_w2, self_w, msg_w, node_b[None, :], out_w,
    )


def solution(mesh):
    owned = ("grp", "dev")
    in_specs = (P(owned, None), P(owned, None, None), P(owned, None, None), P(owned, None)) + (P(),) * 10
    return jax.shard_map(shards, mesh=mesh, in_specs=in_specs, out_specs=P(owned, None), check_vma=False)
```

```python
import jax
import jax.numpy as jnp
from jax import lax
from jax.experimental import pallas as pl
from jax.experimental.pallas import tpu as pltpu
from jax.sharding import PartitionSpec as P

MESH = pl.DeviceIdType.MESH
BF16 = jnp.bfloat16
F32 = jnp.float32

XS = 4
ZS = 8
QS = 8
SLOTS = 16
PEERS = XS * QS
CHUNK = PEERS * SLOTS
OWNERS = XS * ZS * QS
NODES = 2048
NETS = 1024
H = 256
FF = 512
TILE = 256
OPERANDS = 14


def dot(a, b):
    return jnp.dot(a, b, preferred_element_type=F32)


def dot_nt(a, b):
    return lax.dot_general(a, b, (((1,), (1,)), ((), ())), preferred_element_type=F32)


def iota(shape, axis):
    return lax.broadcasted_iota(jnp.int32, shape, axis)


def split_ids(ids):
    high = lax.shift_right_logical(ids, 8)
    low = lax.bitwise_and(ids, 255)
    return jnp.concatenate([high, low], axis=0).astype(F32).astype(BF16)


def chunk_digits(digits, plane):
    pin = iota((CHUNK, OWNERS), 0)
    owner = lax.div(pin, QS * SLOTS) * (ZS * QS) + lax.rem(lax.div(pin, SLOTS), QS)
    take = jnp.where(iota((CHUNK, OWNERS), 1) - plane * QS == owner, 1.0, 0.0).astype(BF16)
    spread = dot_nt(take, digits)
    own_slot = lax.rem(iota((CHUNK, 2 * SLOTS), 1), SLOTS) == lax.rem(iota((CHUNK, 2 * SLOTS), 0), SLOTS)
    return jnp.where(own_slot, spread, 0.0).astype(BF16)


def ids_down(digits, plane):
    weights = jnp.where(iota((2 * SLOTS, 128), 0) < SLOTS, 256.0, 1.0).astype(BF16)
    return dot(chunk_digits(digits, plane), weights).astype(jnp.int32)


def ids_across(digits, plane):
    weights = jnp.where(iota((8, 2 * SLOTS), 1) < SLOTS, 256.0, 1.0).astype(BF16)
    return dot_nt(weights, chunk_digits(digits, plane))[0:1, :].astype(jnp.int32)


def select_rows(table, digits, plane, count):
    ids = jnp.concatenate([ids_down(digits, plane)] * (count // 128), axis=1)
    picked = jnp.where(ids == iota((CHUNK, count), 1), 1.0, 0.0).astype(BF16)
    return dot(picked, table).astype(BF16).reshape(PEERS, SLOTS, H)


def members(ids, base, count):
    return jnp.where(ids == iota((count, CHUNK), 0) + base, 1.0, 0.0).astype(BF16)


def layer_kernel(*refs):
    hbm, o_ref, vmem = refs[:OPERANDS], refs[OPERANDS], refs[OPERANDS + 1 : 2 * OPERANDS + 1]
    (
        table, out1, in1, out2, in2, sums_out, sums_in, messages_in, ids_out, ids_in,
        net_acc, up_acc, down_acc, net_inv, node_acc, self_part, node_digits, net_digits, up_digits, down_digits,
        load, send1, recv1, send2, recv2, send_sums, recv_sums, send_messages, recv_messages, send_ids, recv_ids, column_sem,
    ) = refs[2 * OPERANDS + 1 :]
    (
        node_ids, net_ids, counts, x_ref, pin_w1, pin_b1, pin_w2,
        net_w1, net_b1, net_w2, self_w, msg_w, node_b, out_w,
    ) = vmem
    x = lax.axis_index("grp")
    dev = lax.axis_index("dev")
    z = lax.div(dev, QS)
    q = lax.rem(dev, QS)
    place = x * QS + q

    def plane(dz):
        return lax.rem(z + dz + 2 * ZS, ZS)

    up = (x, plane(1) * QS + q)
    down = (x, plane(-1) * QS + q)

    loads = [pltpu.make_async_copy(a, b, load.at[i]) for i, (a, b) in enumerate(zip(hbm, vmem))]
    for copy in loads[:7]:
        copy.start()

    def signal(sem, dx, dz, dq):
        target = (lax.rem(x + dx, XS), plane(dz) * QS + lax.rem(q + dq, QS))
        pl.semaphore_signal(sem, inc=1, device_id=target, device_id_type=MESH)

    barrier = pltpu.get_barrier_semaphore()
    for dz in (4, 3, 5, 2, 6, 1, 7):
        signal(barrier, 0, dz, 0)
    for dx in range(XS):
        for dq in range(QS):
            if dx or dq:
                signal(barrier, dx, 0, dq)

    def rows_of(tile):
        return pl.ds(pl.multiple_of(tile * TILE, TILE), TILE)

    def transform(tile):
        rows = rows_of(tile)
        inner = jax.nn.gelu(dot(x_ref[rows, :], pin_w1[...]) + pin_b1[...])
        table[rows, :] = dot(inner.astype(BF16), pin_w2[...]).astype(BF16)

    for copy in loads[:7]:
        copy.wait()
    node_digits[...] = split_ids(node_ids[...])
    live_ids = jnp.where(iota((SLOTS, OWNERS), 0) < counts[...], net_ids[...], 4095)
    ids_out[...] = live_ids
    net_digits[...] = split_ids(live_ids)
    pl.loop(0, 6)(transform)
    pl.semaphore_wait(barrier, XS * QS - 1 + ZS - 1)
    for dz in (4, 3, 5, 2, 6, 1, 7):
        signal(column_sem, 0, dz, 0)
    pl.loop(6, NODES // TILE)(transform)
    for copy in loads[7:]:
        copy.start()

    def remote(src, dst, send_sem, recv_sem, device):
        return pltpu.make_async_remote_copy(
            src_ref=src, dst_ref=dst, send_sem=send_sem, recv_sem=recv_sem, device_id=device, device_id_type=MESH
        )

    def send_chunk(src, dst, send_sem, recv_sem, kind, tz, own):
        for dx in (2, 1, 3, 0):
            tx = lax.rem(x + dx, XS)
            for dq in (4, 3, 5, 2, 6, 1, 7, 0):
                tq = lax.rem(q + dq, QS)
                copy = remote(
                    src.at[kind, tx * QS + tq], dst.at[kind, place], send_sem.at[kind], recv_sem.at[kind], (tx, tz * QS + tq)
                )
                if dx or dq:
                    copy.start()
                else:
                    pl.when(jnp.logical_not(own))(copy.start)
                    pl.when(own)(pltpu.make_async_copy(src.at[kind, place], dst.at[kind, place], recv_sem.at[kind]).start)

    def wait_in(dst, recv_sem, kind):
        pltpu.make_async_copy(dst.at[kind], dst.at[kind], recv_sem.at[kind]).wait()

    def gather_nodes(kind):
        out1[kind] = select_rows(table[...], node_digits[...], plane(kind), NODES)

    @pl.loop(0, 3)
    def _(j):
        far = 3 - j
        gather_nodes(far)

        @pl.when(j == 0)
        def _():
            pl.semaphore_wait(column_sem, ZS - 1)

        send_chunk(out1, in1, send1, recv1, far, plane(far - 1), j == 2)
        gather_nodes(ZS - far)
        send_chunk(out1, in1, send1, recv1, ZS - far, plane(1 - far), j == 2)

    id_copies = (
        remote(ids_out, ids_in.at[0], send_ids.at[0], recv_ids.at[0], up),
        remote(ids_out, ids_in.at[1], send_ids.at[1], recv_ids.at[1], down),
    )
    for copy in id_copies:
        copy.start()

    @pl.loop(0, 2)
    def _(j):
        kind = 4 - 4 * j
        gather_nodes(kind)
        send_chunk(out1, in1, send1, recv1, kind, plane(kind), j == 1)

    up_acc[...] = jnp.zeros_like(up_acc)
    down_acc[...] = jnp.zeros_like(down_acc)
    net_acc[...] = jnp.zeros_like(net_acc)
    net_inv[...] = jnp.zeros_like(net_inv)
    ones = jnp.ones((CHUNK, 128), BF16)

    @pl.loop(0, ZS)
    def _(part):
        net_inv[...] += dot(members(ids_across(net_digits[...], part), 0, NETS), ones)

    net_inv[...] = 1.0 / net_inv[...]
    for copy in id_copies:
        copy.wait_recv()
    down_digits[...] = split_ids(ids_in[0])
    up_digits[...] = split_ids(ids_in[1])

    def add_nets(acc, digits, kind, from_plane):
        picked = members(ids_across(digits[...], from_plane), 0, NETS)
        wait_in(in1, recv1, kind)
        acc[...] += dot(picked, in1[kind].reshape(CHUNK, H))

    @pl.loop(0, 3)
    def _(j):
        far = 3 - j
        add_nets(up_acc, up_digits, far, plane(1 - far))
        add_nets(down_acc, down_digits, ZS - far, plane(far - 1))

    sums_out[0] = up_acc[...].astype(BF16)
    sums_out[1] = down_acc[...].astype(BF16)
    sum_copies = (
        remote(sums_out.at[0], sums_in.at[0], send_sums.at[0], recv_sums.at[0], up),
        remote(sums_out.at[1], sums_in.at[1], send_sums.at[1], recv_sums.at[1], down),
    )
    for copy in sum_copies:
        copy.start()

    for copy in loads[7:]:
        copy.wait()
    node_acc[...] = jnp.zeros_like(node_acc)

    @pl.loop(0, NODES // TILE)
    def _(tile):
        rows = rows_of(tile)
        self_part[rows, :] = dot(x_ref[rows, :], self_w[...]) + node_b[...]

    @pl.loop(0, 2)
    def _(j):
        kind = 4 * j
        add_nets(net_acc, net_digits, kind, plane(-kind))

    for copy in sum_copies:
        copy.wait_recv()

    def message_copies(rows):
        return (
            remote(table.at[rows, :], messages_in.at[0, rows, :], send_messages.at[0], recv_messages.at[0], up),
            remote(table.at[rows, :], messages_in.at[1, rows, :], send_messages.at[1], recv_messages.at[1], down),
        )

    @pl.loop(0, NETS // TILE)
    def _(tile):
        rows = rows_of(tile)
        inv = net_inv[rows, :]
        total = net_acc[rows, :] + sums_in[0, rows, :].astype(F32) + sums_in[1, rows, :].astype(F32)
        mean = (total * jnp.concatenate([inv, inv], axis=1)).astype(BF16)
        inner = jax.nn.gelu(dot(mean, net_w1[...]) + net_b1[...])
        table[rows, :] = dot(inner.astype(BF16), net_w2[...]).astype(BF16)
        for copy in message_copies(rows):
            copy.start()

    @pl.loop(0, 2)
    def _(j):
        kind = 4 - 4 * j
        out2[kind] = select_rows(table[pl.ds(0, NETS), :], net_digits[...], plane(kind), NETS)
        send_chunk(out2, in2, send2, recv2, kind, plane(kind), j == 1)

    for copy in message_copies(pl.ds(0, NETS)):
        copy.wait_recv()

    @pl.loop(0, 3)
    def _(j):
        far = 3 - j
        out2[far] = select_rows(messages_in[1], up_digits[...], plane(1 - far), NETS)
        send_chunk(out2, in2, send2, recv2, far, plane(1 - far), j == 2)
        out2[ZS - far] = select_rows(messages_in[0], down_digits[...], plane(far - 1), NETS)
        send_chunk(out2, in2, send2, recv2, ZS - far, plane(far - 1), j == 2)

    def add_nodes(kind):
        ids = ids_across(node_digits[...], plane(kind))
        wait_in(in2, recv2, kind)
        rows = in2[kind].reshape(CHUNK, H)
        for half in range(2):
            part = pl.ds(half * NETS, NETS)
            node_acc[part, :] += dot(members(ids, half * NETS, NETS), rows)

    @pl.loop(0, 2)
    def _(j):
        add_nodes(4 * j)

    @pl.loop(0, 3)
    def _(j):
        add_nodes(3 - j)
        add_nodes(5 + j)

    @pl.loop(0, NODES // TILE)
    def _(tile):
        rows = rows_of(tile)
        pre = self_part[rows, :] + dot(node_acc[rows, :].astype(BF16), msg_w[...])
        inner = (0.5 * pre * (1.0 + jnp.tanh(0.5 * pre))).astype(BF16)
        o_ref[rows, :] = (x_ref[rows, :].astype(F32) + dot(inner, out_w[...])).astype(BF16)

    for src, send_sem in ((out1, send1), (out2, send2)):
        for kind in range(ZS):
            sent = src.at[kind, pl.ds(0, PEERS - 1)] if kind in (0, 1, 7) else src.at[kind]
            pltpu.make_async_copy(sent, sent, send_sem.at[kind]).wait()
    for copy in id_copies + sum_copies + message_copies(pl.ds(0, NETS)):
        copy.wait_send()


def layer(*operands):
    loads = pltpu.SemaphoreType.DMA((OPERANDS,))
    eight = pltpu.SemaphoreType.DMA((ZS,))
    pair = pltpu.SemaphoreType.DMA((2,))
    rows_buf = pltpu.VMEM((ZS, PEERS, SLOTS, H), BF16)
    net_rows = pltpu.VMEM((2, NETS, H), BF16)
    net_sums = pltpu.VMEM((NETS, H), F32)
    digits = pltpu.VMEM((2 * SLOTS, OWNERS), BF16)
    return pl.pallas_call(
        layer_kernel,
        out_shape=jax.ShapeDtypeStruct((NODES, H), BF16),
        in_specs=[pl.BlockSpec(memory_space=pltpu.HBM)] * OPERANDS,
        out_specs=pl.BlockSpec(memory_space=pltpu.VMEM),
        scratch_shapes=[pltpu.VMEM(a.shape, a.dtype) for a in operands]
        + [
            pltpu.VMEM((NODES, H), BF16),
            rows_buf, rows_buf, rows_buf, rows_buf,
            net_rows, net_rows, net_rows,
            pltpu.VMEM((SLOTS, OWNERS), jnp.int32),
            pltpu.VMEM((2, SLOTS, OWNERS), jnp.int32),
            net_sums, net_sums, net_sums,
            pltpu.VMEM((NETS, 128), F32),
            pltpu.VMEM((NODES, H), F32),
            pltpu.VMEM((NODES, FF), F32),
            digits, digits, digits, digits,
            loads, eight, eight, eight, eight, pair, pair, pair, pair, pair, pair,
            pltpu.SemaphoreType.REGULAR,
        ],
        compiler_params=pltpu.CompilerParams(
            collective_id=0, has_side_effects=True, vmem_limit_bytes=56 * 1024 * 1024
        ),
    )(*operands)


def shards(
    node_feat, send_node, pin_net, pin_count,
    pin_w1, pin_b1, pin_w2, net_w1, net_b1, net_w2, self_w, msg_w, node_b, out_w,
):
    return layer(
        send_node[0].T, pin_net[0].T, pin_count, node_feat, pin_w1, pin_b1[None, :], pin_w2,
        net_w1, net_b1[None, :], net_w2, self_w, msg_w, node_b[None, :], out_w,
    )


def solution(mesh):
    owned = ("grp", "dev")
    in_specs = (P(owned, None), P(owned, None, None), P(owned, None, None), P(owned, None)) + (P(),) * 10
    return jax.shard_map(shards, mesh=mesh, in_specs=in_specs, out_specs=P(owned, None), check_vma=False)
```
